32 devices in a mesh: dom: 8 (over z, x), rep: 4 (over y, core).
Axes of the slice: x: 2, y: 2, z: 4, core: 2. Of those that a mesh axis runs over, the one named last changes fastest.
Arguments:
- inputs: bfloat16 [4, 2048, 768], P('rep', 'dom'), may hold values from -6 to 6
- cotangent: bfloat16 [4, 2048, 576], P('rep', 'dom'), may hold values from -6 to 6
- conv_one: bfloat16 [2, 64, 128], replicated, may hold values from -1 to 1
- conv_two: bfloat16 [2, 64, 128], replicated, may hold values from -1 to 1
- mix_weight: bfloat16 [3, 64, 64], replicated, may hold values from -2 to 2
- send_rows: int32 [8, 8, 128], P('dom'), may hold values from 0 to 255, as said below
- counts: int32 [8, 8], P('dom'), may hold values from 0 to 128, as said below
- tile_cols: int32 [16, 12], P('dom'), may hold values from 0 to 9, as said below
- tile_vals: bfloat16 [16, 12, 128, 128], P('dom'), may hold values from -0.15625 to 0.15625
Outputs:
- output: bfloat16 [4, 2048, 576], P('rep', 'dom')
- grad_input: bfloat16 [4, 2048, 768], P('rep', 'dom')
- grad_conv_one: float32 [2, 64, 128], replicated
- grad_conv_two: float32 [2, 64, 128], replicated
- grad_mix: float32 [3, 64, 64], replicated
The draws below stay inside these ranges and needn't reach their ends.
Inputs may be any that keep to these rules, and one draw needn't show every extreme that they name: `send_rows`: rows of the source partition; entries in slots at or beyond counts are arbitrary rows. `counts`: zero for a partition with itself; every partition fills one block completely. `tile_cols`: entries below 2 are own row tiles, entry 2 + q is the block from partition q. Each partition's tiles name each of its own row tiles once and the block from the partition before it; which other blocks are named differs from partition to partition.
All inputs are finite; a program needn't handle non-finite values.
Results may differ from the reference program's by a relative error of at most 0.0075.
Values may be sent and summed in bfloat16 or wider, within the bound.
A program may use at most 128 MiB of HBM per device.

```python
import math
import jax
import jax.numpy as jnp
from jax import lax

C = 64
STEPS = 12
OUT_STEPS = 9
NODE_DEV = 256
BLOCK = 128
NT = 12
PARTS_SIZE = 8
NODES = 2048
WINDOWS = 4
RTILES = 2
CTILES = 10


def draw_send_rows(key, part):
    return jax.random.randint(key, (PARTS_SIZE, PARTS_SIZE, BLOCK), 0, NODE_DEV, dtype=jnp.int32)


def draw_counts(key, part):
    drawn_counts = jax.random.randint(key, (PARTS_SIZE, PARTS_SIZE), 0, BLOCK + 1, dtype=jnp.int32)
    source = jnp.arange(PARTS_SIZE)[:, None]
    target = jnp.arange(PARTS_SIZE)[None, :]
    drawn_counts = jnp.where(target == (source + 1) % PARTS_SIZE, BLOCK, drawn_counts)
    return jnp.where(target == source, 0, drawn_counts).astype(jnp.int32)


def partition_tiles(sub_key, index):
    slot_total = RTILES * NT
    rest_slots = slot_total - RTILES
    order_key, shuffle_key = jax.random.split(sub_key)
    offsets = (1 + jax.random.permutation(order_key, PARTS_SIZE - 1)).astype(jnp.int32)
    offsets = jnp.concatenate([jnp.zeros((1,), jnp.int32), offsets])
    block_order = ((index - 1 - offsets) % PARTS_SIZE).astype(jnp.int32)
    positions = (jnp.arange(rest_slots) % PARTS_SIZE).astype(jnp.int32)
    picked_blocks = jnp.take(block_order, positions)
    slots = jnp.concatenate([jnp.arange(RTILES).astype(jnp.int32), RTILES + picked_blocks])
    shuffle = jax.random.permutation(shuffle_key, slot_total).astype(jnp.int32)
    return jnp.take(slots, shuffle).astype(jnp.int32)


def draw_tile_cols(key, part):
    sub_keys = jax.random.split(jax.random.fold_in(key, 17), PARTS_SIZE)
    indices = jnp.arange(PARTS_SIZE).astype(jnp.int32)
    drawn = jax.vmap(partition_tiles)(sub_keys, indices)
    return drawn.reshape(PARTS_SIZE * RTILES, NT).astype(jnp.int32)


def steps_of(own_key, extent, cuts, least, high):
    def one(position, parts):
        heights = jax.random.uniform(jax.random.fold_in(jax.random.fold_in(own_key, 6), position), (parts,), jnp.float32, least / len(cuts), high / len(cuts))
        return jnp.repeat(jnp.exp(heights), extent[position] // parts).reshape((-1,) + (1,) * (len(extent) - position - 1))

    factor_of = one(*cuts[0])
    for cut in cuts[1:]:
        factor_of = factor_of * one(*cut)
    return factor_of


def normal_values(own_key, shape, deviation, reach, cuts=(), kind=jnp.bfloat16):
    result = jax.random.normal(own_key, shape, jnp.float32) * deviation
    if len(cuts) > 0:
        result = steps_of(own_key, shape, cuts, -0.22, 0.18) * result
    return jnp.clip(result, min=-reach, max=reach).astype(kind)


def setup_inputs(seed: int = 0) -> dict:
    key_list = jax.random.split(jax.random.key(seed), 10)
    return {
        "inputs": normal_values(key_list[0], (WINDOWS, NODES, STEPS * C), 1.0, 6.0, ((0, 4), (1, 8))),
        "cotangent": normal_values(key_list[1], (WINDOWS, NODES, OUT_STEPS * C), 1.0, 6.0, ((0, 4), (1, 8))),
        "conv_one": normal_values(key_list[2], (2, C, 2 * C), (C // 2) ** -0.5, 1.0),
        "conv_two": normal_values(key_list[3], (2, C, 2 * C), (C // 2) ** -0.5, 1.0),
        "mix_weight": normal_values(key_list[4], (3, C, C), (C // 8) ** -0.5, 2.0),
        "send_rows": draw_send_rows(jax.random.fold_in(key_list[9], 71), 0),
        "counts": draw_counts(jax.random.fold_in(key_list[9], 71), 0),
        "tile_cols": draw_tile_cols(jax.random.fold_in(key_list[9], 71), 0),
        "tile_vals": normal_values(key_list[8], (PARTS_SIZE * RTILES, NT, BLOCK, BLOCK), (NT * BLOCK) ** -0.5, 0.15625, ((0, 8),)),
    }


HIGHEST = lax.Precision.HIGHEST

def gated_conv(signal, weight, dilation):
    earlier_steps = signal[:, :-dilation]
    later_steps = signal[:, dilation:]
    preact = jnp.einsum('rsc,co->rso', earlier_steps, weight[0], precision=HIGHEST)
    preact = preact + jnp.einsum('rsc,co->rso', later_steps, weight[1], precision=HIGHEST)
    halfway = weight.shape[1]
    return jnp.tanh(preact[..., :halfway]) * jax.nn.sigmoid(preact[..., halfway:])

def temporal(signal, conv_one, conv_two):
    first = gated_conv(signal, conv_one, 1).astype(jnp.bfloat16)
    first = lax.optimization_barrier(first)
    return gated_conv(first.astype(jnp.float32), conv_two, 2)

def spread(extended, cols, vals):
    row_tiles, count_slots, tile_rows, _ = vals.shape
    blocks = extended.reshape(-1, tile_rows, extended.shape[1])
    summed = jnp.zeros((row_tiles, tile_rows, extended.shape[1]), jnp.float32)
    for slot_index in range(count_slots):
        picked = blocks[cols[:, slot_index]].astype(jnp.float32)
        summed = summed + jnp.einsum('rab,rbm->ram', vals[:, slot_index].astype(jnp.float32), picked, precision=HIGHEST)
    return summed.reshape(row_tiles * tile_rows, -1)

def spread_back(grads, cols, vals, col_tiles):
    row_tiles, count_slots, tile_rows, _ = vals.shape
    blocks = grads.reshape(row_tiles, tile_rows, grads.shape[1]).astype(jnp.float32)
    summed = jnp.zeros((col_tiles, tile_rows, grads.shape[1]), jnp.float32)
    for slot_index in range(count_slots):
        contribution = jnp.einsum('rab,ram->rbm', vals[:, slot_index].astype(jnp.float32), blocks, precision=HIGHEST)
        summed = summed + jax.ops.segment_sum(contribution, cols[:, slot_index], num_segments=col_tiles)
    return summed.reshape(col_tiles * tile_rows, -1)

def partition_rows(values, partitions):
    windows, nodes, feats = values.shape
    shaped = values.reshape(windows, partitions, nodes // partitions, feats).transpose(1, 2, 0, 3)
    return shaped.reshape(partitions, nodes // partitions, windows * feats)

def window_rows(values, windows):
    partitions, local_nodes, merged = values.shape
    shaped = values.reshape(partitions, local_nodes, windows, merged // windows).transpose(2, 0, 1, 3)
    return shaped.reshape(windows, partitions * local_nodes, merged // windows)

def reference(inputs, cotangent, conv_one, conv_two, mix_weight, send_rows, counts, tile_cols, tile_vals):
    windows, nodes, flat = inputs.shape
    channels = mix_weight.shape[1]
    history = flat // channels
    kept_steps = history - 3
    partitions = PARTS_SIZE
    local_nodes = nodes // partitions
    merged = windows * kept_steps * channels
    live_slots = jnp.arange(BLOCK)[None, None, :] < counts[:, :, None]
    cols = tile_cols.reshape(partitions, RTILES, NT)
    vals = tile_vals.reshape(partitions, RTILES, NT, BLOCK, BLOCK)
    every_part = jnp.arange(partitions).astype(jnp.int32)
    signal = inputs.reshape(windows * nodes, history, channels).astype(jnp.float32)
    hidden, pullback = jax.vjp(temporal, signal, conv_one.astype(jnp.float32), conv_two.astype(jnp.float32))
    node_hidden = partition_rows(hidden.astype(jnp.bfloat16).reshape(windows, nodes, kept_steps * channels), partitions)

    def hop(values):
        picked = jax.vmap(lambda table, index: table[index])(values, send_rows)
        sent = jnp.where(live_slots[..., None], picked, jnp.zeros((), values.dtype))

        def one_partition(index):
            halo = lax.dynamic_index_in_dim(sent, index, 1, keepdims=False).reshape(-1, merged)
            extended = jnp.concatenate([values[index], halo], axis=0)
            return spread(extended, cols[index], vals[index])
        return lax.map(one_partition, every_part)

    def hop_back(grads):

        def one_partition(index):
            return spread_back(grads[index], cols[index], vals[index], CTILES)
        ext_grads = lax.map(one_partition, every_part)
        local_part = ext_grads[:, :local_nodes]
        pieces = ext_grads[:, local_nodes:].reshape(partitions, partitions, BLOCK, merged).astype(jnp.bfloat16)

        def gather_to(index):
            piece = lax.dynamic_index_in_dim(pieces, index, 1, keepdims=False).astype(jnp.float32)
            piece = jnp.where(live_slots[index][..., None], piece, 0.0)
            return jax.ops.segment_sum(piece.reshape(-1, merged), send_rows[index].reshape(-1), num_segments=local_nodes)
        return local_part + lax.map(gather_to, every_part)
    first_hop = hop(node_hidden).astype(jnp.bfloat16)
    second_hop = hop(first_hop).astype(jnp.bfloat16)

    def channel_rows(values):
        return values.reshape(partitions, local_nodes, windows * kept_steps, channels).astype(jnp.float32)
    terms = (channel_rows(node_hidden), channel_rows(first_hop), channel_rows(second_hop))
    mix_full = mix_weight.astype(jnp.float32)
    mixed = jnp.einsum('pnkc,cd->pnkd', terms[0], mix_full[0], precision=HIGHEST)
    mixed = mixed + jnp.einsum('pnkc,cd->pnkd', terms[1], mix_full[1], precision=HIGHEST)
    mixed = mixed + jnp.einsum('pnkc,cd->pnkd', terms[2], mix_full[2], precision=HIGHEST)
    residual = channel_rows(partition_rows(inputs[:, :, 3 * channels:], partitions))
    output = window_rows((mixed + residual).astype(jnp.bfloat16).reshape(partitions, local_nodes, merged), windows)
    scaling = math.sqrt(windows * nodes * kept_steps)
    cot_rows = channel_rows(partition_rows(cotangent, partitions))
    grad_mix = jnp.stack([jnp.einsum('pnkc,pnkd->cd', term, cot_rows, precision=HIGHEST) for term in terms]) / scaling

    def through(index):
        return jnp.einsum('pnkd,cd->pnkc', cot_rows, mix_full[index], precision=HIGHEST).reshape(partitions, local_nodes, merged)
    grad_second = through(2).astype(jnp.bfloat16)
    grad_first = (through(1) + hop_back(grad_second)).astype(jnp.bfloat16)
    grad_hidden = through(0) + hop_back(grad_first)
    grad_rows = window_rows(grad_hidden, windows).reshape(windows * nodes, kept_steps, channels)
    grad_signal, grad_one, grad_two = pullback(grad_rows)
    padding = jnp.zeros((windows, nodes, 3 * channels), jnp.float32)
    grad_input = grad_signal.reshape(windows, nodes, flat) + jnp.concatenate([padding, cotangent.astype(jnp.float32)], axis=2)
    return (output, grad_input.astype(jnp.bfloat16), grad_one / scaling, grad_two / scaling, grad_mix)
```

```python
import functools
import math

import jax
import jax.numpy as jnp
from jax import lax
from jax.experimental import pallas as pl
from jax.experimental.pallas import tpu as pltpu
from jax.sharding import PartitionSpec as P

F32 = jnp.float32
BF16 = jnp.bfloat16
BLK = 128
VM = pl.BlockSpec(memory_space=pltpu.VMEM)
SM = pl.BlockSpec(memory_space=pltpu.SMEM)
LIMIT = pltpu.CompilerParams(vmem_limit_bytes=56 * 1024 * 1024)


def dot(a, b):
    return jnp.dot(a, b, preferred_element_type=F32)


def dot_t0(a, b):
    return lax.dot_general(a, b, (((0,), (0,)), ((), ())), preferred_element_type=F32)


def dot_t1(a, b):
    return lax.dot_general(a, b, (((1,), (1,)), ((), ())), preferred_element_type=F32)


def pair(k):
    return slice(k * 128, (k + 1) * 128)


def window2(k):
    return slice(k * 128, (k + 2) * 128)


def block_map(weight_ref, index, out_ref):
    c = weight_ref.shape[1]
    w = weight_ref[index]
    out_ref[...] = jnp.zeros(out_ref.shape, BF16)
    out_ref[0:c, 0:c] = w
    out_ref[c : 2 * c, c : 2 * c] = w


def band_blocks(dilation):
    if dilation == 1:
        return ((0, 1, 0), (0, 2, 1), (1, 2, 0), (1, 3, 1))
    return ((0, 0, 0), (0, 1, 1), (1, 2, 0), (1, 3, 1))


def band_map(conv_ref, dilation, out_ref):
    c = conv_ref.shape[1]
    out_ref[...] = jnp.zeros(out_ref.shape, BF16)
    for tap, i, o in band_blocks(dilation):
        w = conv_ref[tap]
        rows = slice(i * c, (i + 1) * c)
        out_ref[rows, o * c : (o + 1) * c] = w[:, :c]
        out_ref[rows, (o + 2) * c : (o + 3) * c] = w[:, c:]


def band_grad(total, dilation, out_ref):
    c = out_ref.shape[1]
    for tap in range(2):
        for half in range(2):
            acc = None
            for t, i, o in band_blocks(dilation):
                if t != tap:
                    continue
                col = (o + 2 * half) * c
                part = total[i * c : (i + 1) * c, col : col + c]
                acc = part if acc is None else acc + part
            out_ref[tap, :, half * c : (half + 1) * c] = acc


def activations(pre):
    filt = jnp.tanh(pre[:, :128])
    gates = 0.5 * jnp.tanh(0.5 * pre[:, 128:]) + 0.5
    return filt, gates


def earlier(ref, k):
    if k == 0:
        x = ref[:, 0:128]
        return jnp.concatenate([jnp.zeros_like(x), x], axis=1)
    return ref[:, window2(k - 1)]


def build_tiles(cols_ref, vals_ref, acc_ref, dense_ref):
    rtiles, slots = vals_ref.shape[0], vals_ref.shape[1]
    ctiles = dense_ref.shape[1] // BLK
    for r in range(rtiles):
        acc_ref[...] = jnp.zeros(acc_ref.shape, F32)
        for j in range(slots):
            c = cols_ref[r, j]
            acc_ref[c] = acc_ref[c] + vals_ref[r, j].astype(F32)
        for c in range(ctiles):
            dense_ref[r * BLK : (r + 1) * BLK, c * BLK : (c + 1) * BLK] = acc_ref[c].astype(BF16)


def build_picks(send_ref, counts_ref, picks_ref):
    parts = send_ref.shape[0]
    nodes = picks_ref.shape[0]
    lane = lax.broadcasted_iota(jnp.int32, (1, BLK), 1)
    rows = lax.broadcasted_iota(jnp.int32, (nodes, BLK), 0)
    for q in range(parts):
        wanted = jnp.where(lane < counts_ref[0, q], send_ref[q : q + 1, :], -1)
        hit = rows == wanted
        picks_ref[:, q * BLK : (q + 1) * BLK] = jnp.where(hit, 1.0, 0.0).astype(BF16)


def prepare_body(cot_ref, mix_ref, send_ref, counts_ref, cols_ref, vals_ref,
                 dense_ref, picks_ref, cot_out, base_ref, pieces_ref,
                 acc_ref, map_ref, g_ref):
    nodes = cot_ref.shape[0]
    c = mix_ref.shape[1]
    build_tiles(cols_ref, vals_ref, acc_ref, dense_ref)
    build_picks(send_ref, counts_ref, picks_ref)
    wide = cot_ref[...].astype(F32)
    wide = jnp.concatenate([jnp.zeros((nodes, c), F32), wide], axis=1).astype(BF16)
    cot_out[...] = wide
    pairs = cot_out.shape[1] // 128
    block_map(mix_ref, 2, map_ref)
    m = map_ref[...]
    for k in range(pairs):
        g_ref[:, pair(k)] = dot_t1(cot_out[:, pair(k)], m).astype(BF16)
    block_map(mix_ref, 1, map_ref)
    m = map_ref[...]
    g = g_ref[...]
    pieces_ref[...] = dot_t0(dense_ref[:, nodes:], g).astype(BF16)
    base_ref[...] = dot_t0(dense_ref[:, :nodes], g)
    for k in range(pairs):
        base_ref[:, pair(k)] += dot_t1(cot_out[:, pair(k)], m)


def forward_body(x_ref, conv1_ref, conv2_ref, picks_ref, first_ref, hidden_ref, halo_ref,
                 band_ref):
    pairs = x_ref.shape[1] // 128
    band_map(conv1_ref, 1, band_ref)
    b = band_ref[...]
    for k in range(pairs):
        filt, gates = activations(dot(earlier(x_ref, k), b))
        first_ref[:, pair(k)] = (filt * gates).astype(BF16)
    band_map(conv2_ref, 2, band_ref)
    b = band_ref[...]
    for k in range(1, pairs):
        filt, gates = activations(dot(earlier(first_ref, k), b))
        hidden_ref[:, pair(k - 1)] = (filt * gates).astype(BF16)
    halo_ref[...] = dot_t0(picks_ref[...], hidden_ref[...]).astype(BF16)


def back_hop_body(arrived_ref, picks_ref, dense_ref, base_ref, cot_ref, mix_ref,
                  next_base_ref, pieces_ref, map_ref):
    nodes = cot_ref.shape[0]
    pairs = cot_ref.shape[1] // 128
    g = (base_ref[...] + dot(picks_ref[...], arrived_ref[...])).astype(BF16)
    pieces_ref[...] = dot_t0(dense_ref[:, nodes:], g).astype(BF16)
    next_base_ref[...] = dot_t0(dense_ref[:, :nodes], g)
    block_map(mix_ref, 0, map_ref)
    m = map_ref[...]
    for k in range(pairs):
        next_base_ref[:, pair(k)] += dot_t1(cot_ref[:, pair(k)], m)


def hop_body(arrived_ref, picks_ref, dense_ref, hidden_ref, hop_ref, halo_ref):
    nodes = hidden_ref.shape[0]
    total = dot(dense_ref[:, :nodes], hidden_ref[...])
    total = total + dot(dense_ref[:, nodes:], arrived_ref[...])
    hop_ref[...] = total.astype(BF16)
    halo_ref[...] = dot_t0(picks_ref[...], hop_ref[...]).astype(BF16)


def gate_grad(pre, up):
    filt, gates = activations(pre)
    d_filt = up * gates * (1.0 - filt * filt)
    d_gate = up * filt * gates * (1.0 - gates)
    return jnp.concatenate([d_filt, d_gate], axis=1).astype(BF16)


def backward_body(arrived_ref, picks_ref, base_ref, x_ref, first_ref, cot_ref,
                  conv1_ref, conv2_ref, grad_ref, g1_ref, g2_ref,
                  band_ref, up_ref, mid_ref):
    pairs = x_ref.shape[1] // 128
    up_ref[...] = base_ref[...] + dot(picks_ref[...], arrived_ref[...])
    band_map(conv2_ref, 2, band_ref)
    b = band_ref[...]
    total = None
    carry = None
    for k in range(1, pairs):
        both = earlier(first_ref, k)
        d = gate_grad(dot(both, b), up_ref[:, pair(k - 1)])
        part = dot_t0(both, d)
        total = part if total is None else total + part
        back = dot_t1(d, b)
        low = back[:, :128] if carry is None else carry + back[:, :128]
        mid_ref[:, pair(k - 1)] = low.astype(BF16)
        carry = back[:, 128:]
    mid_ref[:, pair(pairs - 1)] = carry.astype(BF16)
    band_grad(total, 2, g2_ref)
    band_map(conv1_ref, 1, band_ref)
    b = band_ref[...]
    total = None
    carry = None
    for k in range(pairs):
        both = earlier(x_ref, k)
        d = gate_grad(dot(both, b), mid_ref[:, pair(k)].astype(F32))
        part = dot_t0(both, d)
        total = part if total is None else total + part
        back = dot_t1(d, b)
        if k > 0:
            low = carry + back[:, :128]
            if k > 1:
                low = low + cot_ref[:, pair(k - 2)].astype(F32)
            grad_ref[:, pair(k - 1)] = low.astype(BF16)
        carry = back[:, 128:]
    last = carry + cot_ref[:, pair(pairs - 2)].astype(F32)
    grad_ref[:, pair(pairs - 1)] = last.astype(BF16)
    band_grad(total, 1, g1_ref)


def finish_body(arrived_ref, dense_ref, hidden_ref, hop_ref, x_ref, cot_ref, mix_ref,
                out_ref, gm_ref, map0, map1, map2, second_ref, wide_ref):
    nodes = hidden_ref.shape[0]
    c = mix_ref.shape[1]
    pairs = hidden_ref.shape[1] // 128
    total = dot(dense_ref[:, :nodes], hop_ref[...])
    total = total + dot(dense_ref[:, nodes:], arrived_ref[...])
    second_ref[...] = total.astype(BF16)
    terms = (hidden_ref, hop_ref, second_ref)
    maps = (map0, map1, map2)
    for i in range(3):
        block_map(mix_ref, i, maps[i])
    for k in range(pairs):
        acc = x_ref[:, pair(k + 1)].astype(F32)
        for term, m in zip(terms, maps):
            acc = acc + dot(term[:, pair(k)], m[...])
        wide_ref[:, pair(k)] = acc
    out_ref[...] = wide_ref[:, c:].astype(BF16)
    for i, term in enumerate(terms):
        acc = None
        for k in range(pairs):
            part = dot_t0(term[:, pair(k)], cot_ref[:, pair(k)])
            acc = part if acc is None else acc + part
        gm_ref[i] = acc[:c, :c] + acc[c:, c:]


def call(body, outs, scratch, ins, specs=None, name=None, flops=0, moved=0):
    return pl.pallas_call(
        body,
        out_shape=[jax.ShapeDtypeStruct(s, d) for s, d in outs],
        in_specs=specs or [VM] * len(ins),
        out_specs=[VM] * len(outs),
        scratch_shapes=[pltpu.VMEM(s, d) for s, d in scratch],
        compiler_params=LIMIT,
        cost_estimate=pl.CostEstimate(flops=flops, bytes_accessed=moved, transcendentals=0),
        name=name,
    )(*ins)


def total_over(values, axes, devices):
    size = values.size
    per = -(-size // devices)
    flat = jnp.pad(values, (0, per * devices - size)).reshape(devices, per)
    got = lax.all_to_all(flat, axes, split_axis=0, concat_axis=0, tiled=True)
    mine = jnp.sum(got, axis=0)
    spread = jnp.broadcast_to(mine[None], (devices, per))
    back = lax.all_to_all(spread, axes, split_axis=0, concat_axis=0, tiled=True)
    return back.reshape(-1)[:size]


def shards(inputs, cotangent, conv_one, conv_two, mix_weight, send_rows, counts, tile_cols,
           tile_vals):
    windows, nodes, flat = inputs.shape
    channels = mix_weight.shape[1]
    parts = lax.axis_size("dom")
    reps = lax.axis_size("rep")
    kept = flat // channels - 3
    wide = flat - 2 * channels
    halo = parts * BLK
    x = inputs[0]
    cot = cotangent[0]
    hop_flops = 4 * nodes * halo * wide
    moved = 2 * halo * wide * 2

    def exchange(v):
        return lax.all_to_all(v, "dom", split_axis=0, concat_axis=0, tiled=True)

    dense, picks, cot_wide, base, pieces = call(
        prepare_body,
        [((nodes, nodes + halo), BF16), ((nodes, halo), BF16), ((nodes, wide), BF16),
         ((nodes, wide), F32), ((halo, wide), BF16)],
        [((parts + nodes // BLK, BLK, BLK), F32), ((128, 128), BF16), ((nodes, wide), BF16)],
        (cot, mix_weight, send_rows[0], counts, tile_cols, tile_vals),
        [VM, VM, VM, SM, SM, VM], "prepare", hop_flops, moved)
    arrived_back = exchange(pieces)
    first, hidden, out_halo = call(
        forward_body,
        [((nodes, flat), BF16), ((nodes, wide), BF16), ((halo, wide), BF16)],
        [((256, 256), BF16)],
        (x, conv_one, conv_two, picks), None, "forward", hop_flops, moved)
    arrived = exchange(out_halo)
    base, pieces = call(
        back_hop_body,
        [((nodes, wide), F32), ((halo, wide), BF16)],
        [((128, 128), BF16)],
        (arrived_back, picks, dense, base, cot_wide, mix_weight), None, "back_hop",
        hop_flops, moved)
    arrived_back = exchange(pieces)
    hop, out_halo = call(
        hop_body,
        [((nodes, wide), BF16), ((halo, wide), BF16)], [],
        (arrived, picks, dense, hidden), None, "hop", hop_flops, moved)
    arrived = exchange(out_halo)
    grad_input, g1, g2 = call(
        backward_body,
        [((nodes, flat), BF16), (conv_one.shape, F32), (conv_two.shape, F32)],
        [((256, 256), BF16), ((nodes, wide), F32), ((nodes, flat), BF16)],
        (arrived_back, picks, base, x, first, cot_wide, conv_one, conv_two), None, "backward",
        hop_flops, moved)
    output, gm = call(
        finish_body,
        [((nodes, kept * channels), BF16), (mix_weight.shape, F32)],
        [((128, 128), BF16)] * 3 + [((nodes, wide), BF16), ((nodes, wide), F32)],
        (arrived, dense, hidden, hop, x, cot_wide, mix_weight), None, "finish",
        hop_flops, moved)
    scaling = math.sqrt(float(windows * reps * nodes * parts * kept))
    packed = jnp.concatenate([g1.reshape(-1), g2.reshape(-1), gm.reshape(-1)])
    packed = total_over(packed, ("dom", "rep"), parts * reps) / scaling
    n1, n2 = g1.size, g2.size
    return (
        output[None],
        grad_input[None],
        packed[:n1].reshape(g1.shape),
        packed[n1 : n1 + n2].reshape(g2.shape),
        packed[n1 + n2 :].reshape(gm.shape),
    )


def solution(mesh):
    placed = (
        P("rep", "dom", None),
        P("rep", "dom", None),
        P(),
        P(),
        P(),
        P("dom", None, None),
        P("dom", None),
        P("dom", None),
        P("dom", None, None, None),
    )
    return jax.shard_map(
        shards,
        mesh=mesh,
        in_specs=placed,
        out_specs=(P("rep", "dom", None), P("rep", "dom", None), P(), P(), P()),
        check_vma=False,
    )
```

```python
import functools
import math

import jax
import jax.numpy as jnp
from jax import lax
from jax.experimental import pallas as pl
from jax.experimental.pallas import tpu as pltpu
from jax.sharding import PartitionSpec as P

F32 = jnp.float32
BF16 = jnp.bfloat16
BLK = 128
VM = pl.BlockSpec(memory_space=pltpu.VMEM)
SM = pl.BlockSpec(memory_space=pltpu.SMEM)
LIMIT = pltpu.CompilerParams(vmem_limit_bytes=56 * 1024 * 1024)


def dot(a, b):
    return jnp.dot(a, b, preferred_element_type=F32)


def dot_t0(a, b):
    return lax.dot_general(a, b, (((0,), (0,)), ((), ())), preferred_element_type=F32)


def dot_t1(a, b):
    return lax.dot_general(a, b, (((1,), (1,)), ((), ())), preferred_element_type=F32)


def pair(k):
    return slice(k * 128, (k + 1) * 128)


def window2(k):
    return slice(k * 128, (k + 2) * 128)


def block_map(weight_ref, index, out_ref):
    c = weight_ref.shape[1]
    w = weight_ref[index]
    out_ref[...] = jnp.zeros(out_ref.shape, BF16)
    out_ref[0:c, 0:c] = w
    out_ref[c : 2 * c, c : 2 * c] = w


def band_blocks(dilation):
    if dilation == 1:
        return ((0, 1, 0), (0, 2, 1), (1, 2, 0), (1, 3, 1))
    return ((0, 0, 0), (0, 1, 1), (1, 2, 0), (1, 3, 1))


def band_map(conv_ref, dilation, out_ref):
    c = conv_ref.shape[1]
    out_ref[...] = jnp.zeros(out_ref.shape, BF16)
    for tap, i, o in band_blocks(dilation):
        w = conv_ref[tap]
        rows = slice(i * c, (i + 1) * c)
        out_ref[rows, o * c : (o + 1) * c] = w[:, :c]
        out_ref[rows, (o + 2) * c : (o + 3) * c] = w[:, c:]


def band_grad(total, dilation, out_ref):
    c = out_ref.shape[1]
    for tap in range(2):
        for half in range(2):
            acc = None
            for t, i, o in band_blocks(dilation):
                if t != tap:
                    continue
                col = (o + 2 * half) * c
                part = total[i * c : (i + 1) * c, col : col + c]
                acc = part if acc is None else acc + part
            out_ref[tap, :, half * c : (half + 1) * c] = acc


def activations(pre):
    filt = jnp.tanh(pre[:, :128])
    gates = 0.5 * jnp.tanh(0.5 * pre[:, 128:]) + 0.5
    return filt, gates


def earlier(ref, k):
    if k == 0:
        x = ref[:, 0:128]
        return jnp.concatenate([jnp.zeros_like(x), x], axis=1)
    return ref[:, window2(k - 1)]


def build_tiles(cols_ref, vals_ref, acc_ref, dense_ref):
    rtiles, slots = vals_ref.shape[0], vals_ref.shape[1]
    ctiles = dense_ref.shape[1] // BLK
    for r in range(rtiles):
        acc_ref[...] = jnp.zeros(acc_ref.shape, F32)
        for j in range(slots):
            c = cols_ref[r, j]
            acc_ref[c] = acc_ref[c] + vals_ref[r, j].astype(F32)
        for c in range(ctiles):
            dense_ref[r * BLK : (r + 1) * BLK, c * BLK : (c + 1) * BLK] = acc_ref[c].astype(BF16)


def build_picks(send_ref, counts_ref, picks_ref):
    parts = send_ref.shape[0]
    nodes = picks_ref.shape[0]
    lane = lax.broadcasted_iota(jnp.int32, (1, BLK), 1)
    rows = lax.broadcasted_iota(jnp.int32, (nodes, BLK), 0)
    for q in range(parts):
        wanted = jnp.where(lane < counts_ref[0, q], send_ref[q : q + 1, :], -1)
        hit = rows == wanted
        picks_ref[:, q * BLK : (q + 1) * BLK] = jnp.where(hit, 1.0, 0.0).astype(BF16)


def prepare_body(cot_ref, mix_ref, send_ref, counts_ref, cols_ref, vals_ref,
                 dense_ref, picks_ref, cot_out, base_ref, pieces_ref,
                 acc_ref, map_ref, g_ref):
    nodes = cot_ref.shape[0]
    parts = send_ref.shape[0]
    c = mix_ref.shape[1]
    build_tiles(cols_ref, vals_ref, acc_ref, dense_ref)
    build_picks(send_ref, counts_ref, picks_ref)
    wide = cot_ref[...].astype(F32)
    wide = jnp.concatenate([jnp.zeros((nodes, c), F32), wide], axis=1).astype(BF16)
    cot_out[...] = wide
    pairs = cot_out.shape[1] // 128
    block_map(mix_ref, 2, map_ref)
    m = map_ref[...]
    for k in range(pairs):
        g_ref[:, pair(k)] = dot_t1(cot_out[:, pair(k)], m).astype(BF16)
    block_map(mix_ref, 1, map_ref)
    m = map_ref[...]
    g = g_ref[...]
    pack_rows(g, dense_ref, nodes, parts, pieces_ref)
    base_ref[...] = dot_t0(dense_ref[:, :nodes], g)
    for k in range(pairs):
        base_ref[:, pair(k)] += dot_t1(cot_out[:, pair(k)], m)


def pack_rows(values, table_ref, start, parts, out_ref):
    flipped = values.astype(F32).T.astype(BF16)
    for q in range(parts):
        table = table_ref[:, start + q * BLK : start + (q + 1) * BLK]
        out_ref[q] = dot(flipped, table).astype(BF16)


def from_blocks(total, table_ref, start, parts, arrived_ref):
    for q in range(parts):
        table = table_ref[:, start + q * BLK : start + (q + 1) * BLK]
        total = total + dot_t1(table, arrived_ref[q])
    return total


def forward_part(x_ref, conv1_ref, conv2_ref, first_ref, hidden_ref, band_ref):
    pairs = x_ref.shape[1] // 128
    band_map(conv1_ref, 1, band_ref)
    b = band_ref[...]
    for k in range(pairs):
        filt, gates = activations(dot(earlier(x_ref, k), b))
        first_ref[:, pair(k)] = (filt * gates).astype(BF16)
    band_map(conv2_ref, 2, band_ref)
    b = band_ref[...]
    for k in range(1, pairs):
        filt, gates = activations(dot(earlier(first_ref, k), b))
        hidden_ref[:, pair(k - 1)] = (filt * gates).astype(BF16)


def gate_grad(pre, up):
    filt, gates = activations(pre)
    d_filt = up * gates * (1.0 - filt * filt)
    d_gate = up * filt * gates * (1.0 - gates)
    return jnp.concatenate([d_filt, d_gate], axis=1).astype(BF16)


def backward_part(x_ref, first_ref, cot_ref, conv1_ref, conv2_ref, grad_ref, g1_ref, g2_ref,
                  band_ref, up_ref, mid_ref):
    pairs = x_ref.shape[1] // 128
    band_map(conv2_ref, 2, band_ref)
    b = band_ref[...]
    total = None
    carry = None
    for k in range(1, pairs):
        both = earlier(first_ref, k)
        d = gate_grad(dot(both, b), up_ref[:, pair(k - 1)])
        part = dot_t0(both, d)
        total = part if total is None else total + part
        back = dot_t1(d, b)
        low = back[:, :128] if carry is None else carry + back[:, :128]
        mid_ref[:, pair(k - 1)] = low.astype(BF16)
        carry = back[:, 128:]
    mid_ref[:, pair(pairs - 1)] = carry.astype(BF16)
    band_grad(total, 2, g2_ref)
    band_map(conv1_ref, 1, band_ref)
    b = band_ref[...]
    total = None
    carry = None
    for k in range(pairs):
        both = earlier(x_ref, k)
        d = gate_grad(dot(both, b), mid_ref[:, pair(k)].astype(F32))
        part = dot_t0(both, d)
        total = part if total is None else total + part
        back = dot_t1(d, b)
        if k > 0:
            low = carry + back[:, :128]
            if k > 1:
                low = low + cot_ref[:, pair(k - 2)].astype(F32)
            grad_ref[:, pair(k - 1)] = low.astype(BF16)
        carry = back[:, 128:]
    last = carry + cot_ref[:, pair(pairs - 2)].astype(F32)
    grad_ref[:, pair(pairs - 1)] = last.astype(BF16)
    band_grad(total, 1, g1_ref)


def finish_part(hidden_ref, hop_ref, second_ref, x_ref, cot_ref, mix_ref,
                out_ref, gm_ref, map0, map1, map2, wide_ref):
    c = mix_ref.shape[1]
    pairs = hidden_ref.shape[1] // 128
    terms = (hidden_ref, hop_ref, second_ref)
    maps = (map0, map1, map2)
    for i in range(3):
        block_map(mix_ref, i, maps[i])
    for k in range(pairs):
        acc = x_ref[:, pair(k + 1)].astype(F32)
        for term, m in zip(terms, maps):
            acc = acc + dot(term[:, pair(k)], m[...])
        wide_ref[:, pair(k)] = acc
    out_ref[...] = wide_ref[:, c:].astype(BF16)
    for i, term in enumerate(terms):
        acc = None
        for k in range(pairs):
            part = dot_t0(term[:, pair(k)], cot_ref[:, pair(k)])
            acc = part if acc is None else acc + part
        gm_ref[i] = acc[:c, :c] + acc[c:, c:]


def main_body(parts, reps, scale,
              x_ref, cot_ref, conv1_ref, conv2_ref, mix_ref, dense_ref, picks_ref, base_ref,
              pieces_ref,
              out_ref, grad_ref, o1_ref, o2_ref, om_ref,
              first_ref, hidden_ref, hop_ref, second_ref, up_ref, mid_ref, band_ref,
              map0, map1, map2, g1_ref, g2_ref, gm_ref,
              send1, send2, send3, recv0, recv1, recv2, recv3,
              pack_ref, got_ref, part_ref, reps_ref, sums_ref,
              ssem, rsem, asem, arsem, bsem, brsem):
    me = lax.axis_index("dom")
    mine = lax.axis_index("rep")
    nodes = x_ref.shape[0]
    c = mix_ref.shape[1]
    pairs = cot_ref.shape[1] // 128
    feats = cot_ref.shape[1]

    barrier = pltpu.get_barrier_semaphore()
    for o in range(1, parts):
        pl.semaphore_signal(barrier, inc=1, device_id={"dom": lax.rem(me + o, parts)},
                            device_id_type=pl.DeviceIdType.MESH)
    for o in range(1, reps):
        pl.semaphore_signal(barrier, inc=1, device_id={"rep": lax.rem(mine + o, reps)},
                            device_id_type=pl.DeviceIdType.MESH)
    pl.semaphore_wait(barrier, parts - 1 + reps - 1)

    def copies(level, src, dst):
        made = []
        for o in range(1, parts):
            peer = lax.rem(me + o, parts)
            made.append(pltpu.make_async_remote_copy(
                src_ref=src.at[peer, pl.ds(c, feats - c)],
                dst_ref=dst.at[me, pl.ds(c, feats - c)],
                send_sem=ssem.at[level, o],
                recv_sem=rsem.at[level, o],
                device_id={"dom": peer},
                device_id_type=pl.DeviceIdType.MESH,
            ))
        for m in made:
            m.start()
        return made

    def arrive(made):
        for m in made:
            m.wait_recv()

    round0 = copies(0, pieces_ref, recv0)
    for buf in (recv0, recv1, recv2, recv3):
        buf[:, 0:c, :] = jnp.zeros((parts, c, BLK), BF16)
        buf[me] = jnp.zeros((feats, BLK), BF16)

    forward_part(x_ref, conv1_ref, conv2_ref, first_ref, hidden_ref, band_ref)
    pack_rows(hidden_ref[...], picks_ref, 0, parts, send1)
    round1 = copies(1, send1, recv1)

    arrive(round0)
    g = from_blocks(base_ref[...], picks_ref, 0, parts, recv0).astype(BF16)
    pack_rows(g, dense_ref, nodes, parts, send2)
    round2 = copies(2, send2, recv2)
    up_ref[...] = dot_t0(dense_ref[:, :nodes], g)
    block_map(mix_ref, 0, map0)
    for k in range(pairs):
        up_ref[:, pair(k)] += dot_t1(cot_ref[:, pair(k)], map0[...])

    own = dot(dense_ref[:, :nodes], hidden_ref[...])
    arrive(round1)
    hop_ref[...] = from_blocks(own, dense_ref, nodes, parts, recv1).astype(BF16)
    pack_rows(hop_ref[...], picks_ref, 0, parts, send3)
    round3 = copies(3, send3, recv3)

    arrive(round2)
    up_ref[...] = from_blocks(up_ref[...], picks_ref, 0, parts, recv2)
    backward_part(x_ref, first_ref, cot_ref, conv1_ref, conv2_ref, grad_ref, g1_ref, g2_ref,
                  band_ref, up_ref, mid_ref)

    own = dot(dense_ref[:, :nodes], hop_ref[...])
    arrive(round3)
    second_ref[...] = from_blocks(own, dense_ref, nodes, parts, recv3).astype(BF16)
    finish_part(hidden_ref, hop_ref, second_ref, x_ref, cot_ref, mix_ref, out_ref, gm_ref,
                map0, map1, map2, up_ref)
    for made in (round0, round1, round2, round3):
        for m in made:
            m.wait_send()

    per = pack_ref.shape[1]
    flat = pack_ref
    flat[...] = jnp.zeros(flat.shape, F32)

    def put(first_row, value):
        rows = value.shape[0]
        done = 0
        while done < rows:
            slot, at = divmod(first_row + done, per)
            step = min(per - at, rows - done)
            flat[slot, at : at + step, :] = value[done : done + step]
            done += step

    put(0, g1_ref[0])
    put(c, g1_ref[1])
    put(2 * c, g2_ref[0])
    put(3 * c, g2_ref[1])
    put(4 * c, jnp.concatenate([gm_ref[0], gm_ref[1]], axis=1))
    put(5 * c, jnp.concatenate([gm_ref[2], jnp.zeros((c, c), F32)], axis=1))

    scatter = []
    for o in range(1, parts):
        peer = lax.rem(me + o, parts)
        scatter.append(pltpu.make_async_remote_copy(
            src_ref=pack_ref.at[peer], dst_ref=got_ref.at[me],
            send_sem=asem.at[0, o], recv_sem=arsem.at[0, o],
            device_id={"dom": peer}, device_id_type=pl.DeviceIdType.MESH))
    for m in scatter:
        m.start()
    got_ref[me] = pack_ref[me]
    arrive(scatter)
    total = got_ref[0]
    for q in range(1, parts):
        total = total + got_ref[q]
    part_ref[...] = total
    around = []
    for o in range(1, reps):
        peer = lax.rem(mine + o, reps)
        around.append(pltpu.make_async_remote_copy(
            src_ref=part_ref, dst_ref=reps_ref.at[mine],
            send_sem=bsem.at[o], recv_sem=brsem.at[o],
            device_id={"rep": peer}, device_id_type=pl.DeviceIdType.MESH))
    for m in around:
        m.start()
    reps_ref[mine] = total
    arrive(around)
    total = reps_ref[0]
    for q in range(1, reps):
        total = total + reps_ref[q]
    for m in around:
        m.wait_send()
    part_ref[...] = total * (1.0 / scale)
    final = []
    for o in range(1, parts):
        peer = lax.rem(me + o, parts)
        final.append(pltpu.make_async_remote_copy(
            src_ref=part_ref, dst_ref=sums_ref.at[me],
            send_sem=asem.at[1, o], recv_sem=arsem.at[1, o],
            device_id={"dom": peer}, device_id_type=pl.DeviceIdType.MESH))
    for m in final:
        m.start()
    sums_ref[me] = part_ref[...]
    arrive(final)

    def take(first_row, rows):
        found = []
        done = 0
        while done < rows:
            slot, at = divmod(first_row + done, per)
            step = min(per - at, rows - done)
            found.append(sums_ref[slot, at : at + step, :])
            done += step
        return jnp.concatenate(found, axis=0) if len(found) > 1 else found[0]

    o1_ref[0] = take(0, c)
    o1_ref[1] = take(c, c)
    o2_ref[0] = take(2 * c, c)
    o2_ref[1] = take(3 * c, c)
    both = take(4 * c, c)
    om_ref[0] = both[:, :c]
    om_ref[1] = both[:, c:]
    om_ref[2] = take(5 * c, c)[:, :c]
    for m in scatter + final:
        m.wait_send()


def shards(inputs, cotangent, conv_one, conv_two, mix_weight, send_rows, counts, tile_cols,
           tile_vals):
    windows, nodes, flat = inputs.shape
    channels = mix_weight.shape[1]
    parts = lax.axis_size("dom")
    reps = lax.axis_size("rep")
    kept = flat // channels - 3
    wide = flat - 2 * channels
    halo = parts * BLK
    blocks = (parts, wide, BLK)
    prepared = [((nodes, nodes + halo), BF16), ((nodes, halo), BF16), ((nodes, wide), BF16),
                ((nodes, wide), F32), (blocks, BF16)]
    dense, picks, cot_wide, base, pieces = pl.pallas_call(
        prepare_body,
        out_shape=[jax.ShapeDtypeStruct(s, d) for s, d in prepared],
        in_specs=[VM, VM, VM, SM, SM, VM],
        out_specs=[VM] * 5,
        scratch_shapes=[pltpu.VMEM((parts + nodes // BLK, BLK, BLK), F32),
                        pltpu.VMEM((128, 128), BF16), pltpu.VMEM((nodes, wide), BF16)],
        compiler_params=LIMIT,
        name="prepare",
    )(cotangent[0], mix_weight, send_rows[0], counts, tile_cols, tile_vals)
    scaling = math.sqrt(float(windows * reps * nodes * parts * kept))
    unit = 8 * parts
    per = -(-6 * channels // unit) * unit // parts
    results = [((nodes, kept * channels), BF16), ((nodes, flat), BF16), (conv_one.shape, F32),
               (conv_two.shape, F32), (mix_weight.shape, F32)]
    scratch = [((nodes, flat), BF16), ((nodes, wide), BF16), ((nodes, wide), BF16),
               ((nodes, wide), BF16), ((nodes, wide), F32), ((nodes, flat), BF16),
               ((256, 256), BF16), ((128, 128), BF16), ((128, 128), BF16), ((128, 128), BF16),
               (conv_one.shape, F32), (conv_two.shape, F32), (mix_weight.shape, F32)]
    scratch += [(blocks, BF16)] * 7
    scratch += [((parts, per, BLK), F32), ((parts, per, BLK), F32), ((per, BLK), F32),
                ((reps, per, BLK), F32), ((parts, per, BLK), F32)]
    dma = pltpu.SemaphoreType.DMA
    output, grad_input, g1, g2, gm = pl.pallas_call(
        functools.partial(main_body, parts, reps, scaling),
        out_shape=[jax.ShapeDtypeStruct(s, d) for s, d in results],
        in_specs=[VM] * 9,
        out_specs=[VM] * 5,
        scratch_shapes=[pltpu.VMEM(s, d) for s, d in scratch]
        + [dma((4, parts)), dma((4, parts)), dma((2, parts)), dma((2, parts)), dma((reps,)),
           dma((reps,))],
        compiler_params=pltpu.CompilerParams(
            vmem_limit_bytes=60 * 1024 * 1024, collective_id=0, has_side_effects=True),
        name="layer",
    )(inputs[0], cot_wide, conv_one, conv_two, mix_weight, dense, picks, base, pieces)
    return output[None], grad_input[None], g1, g2, gm


def solution(mesh):
    placed = (
        P("rep", "dom", None),
        P("rep", "dom", None),
        P(),
        P(),
        P(),
        P("dom", None, None),
        P("dom", None),
        P("dom", None),
        P("dom", None, None, None),
    )
    return jax.shard_map(
        shards,
        mesh=mesh,
        in_specs=placed,
        out_specs=(P("rep", "dom", None), P("rep", "dom", None), P(), P(), P()),
        check_vma=False,
    )
```

```python
import functools
import math

import jax
import jax.numpy as jnp
from jax import lax
from jax.experimental import pallas as pl
from jax.experimental.pallas import tpu as pltpu
from jax.sharding import PartitionSpec as P

F32 = jnp.float32
BF16 = jnp.bfloat16
BLK = 128
VM = pl.BlockSpec(memory_space=pltpu.VMEM)
SM = pl.BlockSpec(memory_space=pltpu.SMEM)
LIMIT = pltpu.CompilerParams(vmem_limit_bytes=56 * 1024 * 1024)


def dot(a, b):
    return jnp.dot(a, b, preferred_element_type=F32)


def dot_t0(a, b):
    return lax.dot_general(a, b, (((0,), (0,)), ((), ())), preferred_element_type=F32)


def dot_t1(a, b):
    return lax.dot_general(a, b, (((1,), (1,)), ((), ())), preferred_element_type=F32)


def pair(k):
    return slice(k * 128, (k + 1) * 128)


def window2(k):
    return slice(k * 128, (k + 2) * 128)


def block_map(weight_ref, index, out_ref):
    c = weight_ref.shape[1]
    w = weight_ref[index]
    out_ref[...] = jnp.zeros(out_ref.shape, BF16)
    out_ref[0:c, 0:c] = w
    out_ref[c : 2 * c, c : 2 * c] = w


def band_blocks(dilation):
    if dilation == 1:
        return ((0, 1, 0), (0, 2, 1), (1, 2, 0), (1, 3, 1))
    return ((0, 0, 0), (0, 1, 1), (1, 2, 0), (1, 3, 1))


def band_map(conv_ref, dilation, out_ref):
    c = conv_ref.shape[1]
    out_ref[...] = jnp.zeros(out_ref.shape, BF16)
    for tap, i, o in band_blocks(dilation):
        w = conv_ref[tap]
        rows = slice(i * c, (i + 1) * c)
        out_ref[rows, o * c : (o + 1) * c] = w[:, :c]
        out_ref[rows, (o + 2) * c : (o + 3) * c] = w[:, c:]


def band_grad(total, dilation, out_ref):
    c = out_ref.shape[1]
    for tap in range(2):
        for half in range(2):
            acc = None
            for t, i, o in band_blocks(dilation):
                if t != tap:
                    continue
                col = (o + 2 * half) * c
                part = total[i * c : (i + 1) * c, col : col + c]
                acc = part if acc is None else acc + part
            out_ref[tap, :, half * c : (half + 1) * c] = acc


def activations(pre):
    filt = jnp.tanh(pre[:, :128])
    gates = 0.5 * jnp.tanh(0.5 * pre[:, 128:]) + 0.5
    return filt, gates


def earlier(ref, k):
    if k == 0:
        x = ref[:, 0:128]
        return jnp.concatenate([jnp.zeros_like(x), x], axis=1)
    return ref[:, window2(k - 1)]


def build_tiles(cols_ref, vals_ref, acc_ref, dense_ref):
    rtiles, slots = vals_ref.shape[0], vals_ref.shape[1]
    ctiles = dense_ref.shape[1] // BLK
    for r in range(rtiles):
        acc_ref[...] = jnp.zeros(acc_ref.shape, F32)
        for j in range(slots):
            c = cols_ref[r, j]
            acc_ref[c] = acc_ref[c] + vals_ref[r, j].astype(F32)
        for c in range(ctiles):
            dense_ref[r * BLK : (r + 1) * BLK, c * BLK : (c + 1) * BLK] = acc_ref[c].astype(BF16)


def build_picks(send_ref, counts_ref, picks_ref):
    parts = send_ref.shape[0]
    nodes = picks_ref.shape[0]
    lane = lax.broadcasted_iota(jnp.int32, (1, BLK), 1)
    rows = lax.broadcasted_iota(jnp.int32, (nodes, BLK), 0)
    for q in range(parts):
        wanted = jnp.where(lane < counts_ref[0, q], send_ref[q : q + 1, :], -1)
        hit = rows == wanted
        picks_ref[:, q * BLK : (q + 1) * BLK] = jnp.where(hit, 1.0, 0.0).astype(BF16)


def prepare_body(cot_ref, mix_ref, send_ref, counts_ref, cols_ref, vals_ref,
                 dense_ref, picks_ref, cot_out, base_ref, pieces_ref,
                 acc_ref, map_ref, g_ref):
    nodes = cot_ref.shape[1]
    parts = send_ref.shape[0]
    c = mix_ref.shape[1]
    build_tiles(cols_ref, vals_ref, acc_ref, dense_ref)
    build_picks(send_ref, counts_ref, picks_ref)
    wide = cot_ref[...].astype(F32).T
    wide = jnp.concatenate([jnp.zeros((nodes, c), F32), wide], axis=1).astype(BF16)
    cot_out[...] = wide
    pairs = cot_out.shape[1] // 128
    block_map(mix_ref, 2, map_ref)
    m = map_ref[...]
    for k in range(pairs):
        g_ref[:, pair(k)] = dot_t1(cot_out[:, pair(k)], m).astype(BF16)
    block_map(mix_ref, 1, map_ref)
    m = map_ref[...]
    g = g_ref[...]
    pack_rows(g, dense_ref, nodes, parts, pieces_ref)
    base_ref[...] = dot_t0(dense_ref[:, :nodes], g)
    for k in range(pairs):
        base_ref[:, pair(k)] += dot_t1(cot_out[:, pair(k)], m)


def pack_rows(values, table_ref, start, parts, out_ref):
    flipped = values.astype(F32).T.astype(BF16)
    for q in range(parts):
        table = table_ref[:, start + q * BLK : start + (q + 1) * BLK]
        out_ref[q] = dot(flipped, table).astype(BF16)


def from_blocks(total, table_ref, start, parts, arrived_ref):
    for q in range(parts):
        table = table_ref[:, start + q * BLK : start + (q + 1) * BLK]
        total = total + dot_t1(table, arrived_ref[q])
    return total


def forward_part(x_ref, conv1_ref, conv2_ref, first_ref, hidden_ref, band_ref):
    pairs = x_ref.shape[1] // 128
    band_map(conv1_ref, 1, band_ref)
    b = band_ref[...]
    for k in range(pairs):
        filt, gates = activations(dot(earlier(x_ref, k), b))
        first_ref[:, pair(k)] = (filt * gates).astype(BF16)
    band_map(conv2_ref, 2, band_ref)
    b = band_ref[...]
    for k in range(1, pairs):
        filt, gates = activations(dot(earlier(first_ref, k), b))
        hidden_ref[:, pair(k - 1)] = (filt * gates).astype(BF16)


def gate_grad(pre, up):
    filt, gates = activations(pre)
    d_filt = up * gates * (1.0 - filt * filt)
    d_gate = up * filt * gates * (1.0 - gates)
    return jnp.concatenate([d_filt, d_gate], axis=1).astype(BF16)


def backward_part(x_ref, first_ref, cot_ref, conv1_ref, conv2_ref, grad_ref, g1_ref, g2_ref,
                  band_ref, up_ref, mid_ref):
    pairs = x_ref.shape[1] // 128
    band_map(conv2_ref, 2, band_ref)
    b = band_ref[...]
    total = None
    carry = None
    for k in range(1, pairs):
        both = earlier(first_ref, k)
        d = gate_grad(dot(both, b), up_ref[:, pair(k - 1)])
        part = dot_t0(both, d)
        total = part if total is None else total + part
        back = dot_t1(d, b)
        low = back[:, :128] if carry is None else carry + back[:, :128]
        mid_ref[:, pair(k - 1)] = low.astype(BF16)
        carry = back[:, 128:]
    mid_ref[:, pair(pairs - 1)] = carry.astype(BF16)
    band_grad(total, 2, g2_ref)
    band_map(conv1_ref, 1, band_ref)
    b = band_ref[...]
    total = None
    carry = None
    for k in range(pairs):
        both = earlier(x_ref, k)
        d = gate_grad(dot(both, b), mid_ref[:, pair(k)].astype(F32))
        part = dot_t0(both, d)
        total = part if total is None else total + part
        back = dot_t1(d, b)
        if k > 0:
            low = carry + back[:, :128]
            if k > 1:
                low = low + cot_ref[:, pair(k - 2)].astype(F32)
            grad_ref[:, pair(k - 1)] = low.astype(BF16)
        carry = back[:, 128:]
    last = carry + cot_ref[:, pair(pairs - 2)].astype(F32)
    grad_ref[:, pair(pairs - 1)] = last.astype(BF16)
    band_grad(total, 1, g1_ref)


def mix_grad(term_ref, cot_ref, c):
    acc = None
    for k in range(cot_ref.shape[1] // 128):
        part = dot_t0(term_ref[:, pair(k)], cot_ref[:, pair(k)])
        acc = part if acc is None else acc + part
    return acc[:c, :c] + acc[c:, c:]


def early_part(hidden_ref, hop_ref, x_ref, cot_ref, mix_ref, gm_ref, map0, map1, wide_ref):
    c = mix_ref.shape[1]
    block_map(mix_ref, 0, map0)
    block_map(mix_ref, 1, map1)
    for k in range(cot_ref.shape[1] // 128):
        acc = x_ref[:, pair(k + 1)].astype(F32)
        acc = acc + dot(hidden_ref[:, pair(k)], map0[...])
        wide_ref[:, pair(k)] = acc + dot(hop_ref[:, pair(k)], map1[...])
    gm_ref[0] = mix_grad(hidden_ref, cot_ref, c)
    gm_ref[1] = mix_grad(hop_ref, cot_ref, c)


def main_body(parts, reps, scale,
              x_ref, cot_ref, conv1_ref, conv2_ref, mix_ref, dense_ref, picks_ref, base_ref,
              pieces_ref,
              out_ref, grad_ref, o1_ref, o2_ref, om_ref,
              first_ref, hidden_ref, hop_ref, second_ref, up_ref, mid_ref, band_ref,
              map0, map1, map2, g1_ref, g2_ref, gm_ref,
              wide_ref, send1, send2, send3, recv0, recv1, recv2, recv3,
              pack_ref, got_ref, part_ref, reps_ref, sums_ref,
              ssem, rsem, asem, arsem, bsem, brsem):
    me = lax.axis_index("dom")
    mine = lax.axis_index("rep")
    nodes = x_ref.shape[0]
    c = mix_ref.shape[1]
    pairs = cot_ref.shape[1] // 128
    feats = cot_ref.shape[1]

    barrier = pltpu.get_barrier_semaphore()
    for o in range(1, parts):
        pl.semaphore_signal(barrier, inc=1, device_id={"dom": lax.rem(me + o, parts)},
                            device_id_type=pl.DeviceIdType.MESH)
    for o in range(1, reps):
        pl.semaphore_signal(barrier, inc=1, device_id={"rep": lax.rem(mine + o, reps)},
                            device_id_type=pl.DeviceIdType.MESH)
    pl.semaphore_wait(barrier, parts - 1 + reps - 1)

    def copies(level, src, dst):
        made = []
        for o in sorted(range(1, parts), key=lambda o: abs(2 * o - parts)):
            peer = lax.rem(me + o, parts)
            made.append(pltpu.make_async_remote_copy(
                src_ref=src.at[peer, pl.ds(c, feats - c)],
                dst_ref=dst.at[me, pl.ds(c, feats - c)],
                send_sem=ssem.at[level, o],
                recv_sem=rsem.at[level, o],
                device_id={"dom": peer},
                device_id_type=pl.DeviceIdType.MESH,
            ))
        for m in made:
            m.start()
        return made

    def arrive(made):
        for m in made:
            m.wait_recv()

    round0 = copies(0, pieces_ref, recv0)
    for buf in (recv0, recv1, recv2, recv3):
        buf[:, 0:c, :] = jnp.zeros((parts, c, BLK), BF16)
        buf[me] = jnp.zeros((feats, BLK), BF16)

    forward_part(x_ref, conv1_ref, conv2_ref, first_ref, hidden_ref, band_ref)
    pack_rows(hidden_ref[...], picks_ref, 0, parts, send1)
    round1 = copies(1, send1, recv1)

    arrive(round0)
    g = from_blocks(base_ref[...], picks_ref, 0, parts, recv0).astype(BF16)
    pack_rows(g, dense_ref, nodes, parts, send2)
    round2 = copies(2, send2, recv2)
    up_ref[...] = dot_t0(dense_ref[:, :nodes], g)
    block_map(mix_ref, 0, map0)
    for k in range(pairs):
        up_ref[:, pair(k)] += dot_t1(cot_ref[:, pair(k)], map0[...])

    own = dot(dense_ref[:, :nodes], hidden_ref[...])
    arrive(round1)
    hop_ref[...] = from_blocks(own, dense_ref, nodes, parts, recv1).astype(BF16)
    pack_rows(hop_ref[...], picks_ref, 0, parts, send3)
    round3 = copies(3, send3, recv3)

    arrive(round2)
    up_ref[...] = from_blocks(up_ref[...], picks_ref, 0, parts, recv2)
    backward_part(x_ref, first_ref, cot_ref, conv1_ref, conv2_ref, grad_ref, g1_ref, g2_ref,
                  band_ref, up_ref, mid_ref)

    early_part(hidden_ref, hop_ref, x_ref, cot_ref, mix_ref, gm_ref, map0, map1, wide_ref)
    block_map(mix_ref, 2, map2)
    own = dot(dense_ref[:, :nodes], hop_ref[...])
    arrive(round3)
    second_ref[...] = from_blocks(own, dense_ref, nodes, parts, recv3).astype(BF16)
    gm_ref[2] = mix_grad(second_ref, cot_ref, c)

    per = pack_ref.shape[1]
    flat = pack_ref
    flat[...] = jnp.zeros(flat.shape, F32)

    def put(first_row, value):
        rows = value.shape[0]
        done = 0
        while done < rows:
            slot, at = divmod(first_row + done, per)
            step = min(per - at, rows - done)
            flat[slot, at : at + step, :] = value[done : done + step]
            done += step

    put(0, g1_ref[0])
    put(c, g1_ref[1])
    put(2 * c, g2_ref[0])
    put(3 * c, g2_ref[1])
    put(4 * c, jnp.concatenate([gm_ref[0], gm_ref[1]], axis=1))
    put(5 * c, jnp.concatenate([gm_ref[2], jnp.zeros((c, c), F32)], axis=1))

    scatter = []
    for o in range(1, parts):
        peer = lax.rem(me + o, parts)
        scatter.append(pltpu.make_async_remote_copy(
            src_ref=pack_ref.at[peer], dst_ref=got_ref.at[me],
            send_sem=asem.at[0, o], recv_sem=arsem.at[0, o],
            device_id={"dom": peer}, device_id_type=pl.DeviceIdType.MESH))
    for m in scatter:
        m.start()
    for k in range(pairs):
        wide_ref[:, pair(k)] += dot(second_ref[:, pair(k)], map2[...])
    out_ref[...] = wide_ref[:, c:].astype(BF16)
    got_ref[me] = pack_ref[me]
    arrive(scatter)
    total = got_ref[0]
    for q in range(1, parts):
        total = total + got_ref[q]
    part_ref[...] = total
    around = []
    for o in range(1, reps):
        peer = lax.rem(mine + o, reps)
        around.append(pltpu.make_async_remote_copy(
            src_ref=part_ref, dst_ref=reps_ref.at[mine],
            send_sem=bsem.at[o], recv_sem=brsem.at[o],
            device_id={"rep": peer}, device_id_type=pl.DeviceIdType.MESH))
    for m in around:
        m.start()
    reps_ref[mine] = total
    arrive(around)
    total = reps_ref[0]
    for q in range(1, reps):
        total = total + reps_ref[q]
    for m in around:
        m.wait_send()
    part_ref[...] = total * (1.0 / scale)
    final = []
    for o in range(1, parts):
        peer = lax.rem(me + o, parts)
        final.append(pltpu.make_async_remote_copy(
            src_ref=part_ref, dst_ref=sums_ref.at[me],
            send_sem=asem.at[1, o], recv_sem=arsem.at[1, o],
            device_id={"dom": peer}, device_id_type=pl.DeviceIdType.MESH))
    for m in final:
        m.start()
    sums_ref[me] = part_ref[...]
    arrive(final)

    def take(first_row, rows):
        found = []
        done = 0
        while done < rows:
            slot, at = divmod(first_row + done, per)
            step = min(per - at, rows - done)
            found.append(sums_ref[slot, at : at + step, :])
            done += step
        return jnp.concatenate(found, axis=0) if len(found) > 1 else found[0]

    o1_ref[0] = take(0, c)
    o1_ref[1] = take(c, c)
    o2_ref[0] = take(2 * c, c)
    o2_ref[1] = take(3 * c, c)
    both = take(4 * c, c)
    om_ref[0] = both[:, :c]
    om_ref[1] = both[:, c:]
    om_ref[2] = take(5 * c, c)[:, :c]
    for m in round0 + round1 + round2 + round3 + scatter + final:
        m.wait_send()


def shards(inputs, cotangent, conv_one, conv_two, mix_weight, send_rows, counts, tile_cols,
           tile_vals):
    windows, nodes, flat = inputs.shape
    channels = mix_weight.shape[1]
    parts = lax.axis_size("dom")
    reps = lax.axis_size("rep")
    kept = flat // channels - 3
    wide = flat - 2 * channels
    halo = parts * BLK
    blocks = (parts, wide, BLK)
    prepared = [((nodes, nodes + halo), BF16), ((nodes, halo), BF16), ((nodes, wide), BF16),
                ((nodes, wide), F32), (blocks, BF16)]
    dense, picks, cot_wide, base, pieces = pl.pallas_call(
        prepare_body,
        out_shape=[jax.ShapeDtypeStruct(s, d) for s, d in prepared],
        in_specs=[VM, VM, VM, SM, SM, VM],
        out_specs=[VM] * 5,
        scratch_shapes=[pltpu.VMEM((parts + nodes // BLK, BLK, BLK), F32),
                        pltpu.VMEM((128, 128), BF16), pltpu.VMEM((nodes, wide), BF16)],
        compiler_params=LIMIT,
        name="prepare",
    )(cotangent[0].T, mix_weight, send_rows[0], counts, tile_cols, tile_vals)
    scaling = math.sqrt(float(windows * reps * nodes * parts * kept))
    unit = 8 * parts
    per = -(-6 * channels // unit) * unit // parts
    results = [((nodes, kept * channels), BF16), ((nodes, flat), BF16), (conv_one.shape, F32),
               (conv_two.shape, F32), (mix_weight.shape, F32)]
    scratch = [((nodes, flat), BF16), ((nodes, wide), BF16), ((nodes, wide), BF16),
               ((nodes, wide), BF16), ((nodes, wide), F32), ((nodes, flat), BF16),
               ((256, 256), BF16), ((128, 128), BF16), ((128, 128), BF16), ((128, 128), BF16),
               (conv_one.shape, F32), (conv_two.shape, F32), (mix_weight.shape, F32)]
    scratch += [((nodes, wide), F32)] + [(blocks, BF16)] * 7
    scratch += [((parts, per, BLK), F32), ((parts, per, BLK), F32), ((per, BLK), F32),
                ((reps, per, BLK), F32), ((parts, per, BLK), F32)]
    dma = pltpu.SemaphoreType.DMA
    output, grad_input, g1, g2, gm = pl.pallas_call(
        functools.partial(main_body, parts, reps, scaling),
        out_shape=[jax.ShapeDtypeStruct(s, d) for s, d in results],
        in_specs=[VM] * 9,
        out_specs=[VM] * 5,
        scratch_shapes=[pltpu.VMEM(s, d) for s, d in scratch]
        + [dma((4, parts)), dma((4, parts)), dma((2, parts)), dma((2, parts)), dma((reps,)),
           dma((reps,))],
        compiler_params=pltpu.CompilerParams(
            vmem_limit_bytes=60 * 1024 * 1024, collective_id=0, has_side_effects=True),
        name="layer",
    )(inputs[0], cot_wide, conv_one, conv_two, mix_weight, dense, picks, base, pieces)
    return output[None], grad_input[None], g1, g2, gm


def solution(mesh):
    placed = (
        P("rep", "dom", None),
        P("rep", "dom", None),
        P(),
        P(),
        P(),
        P("dom", None, None),
        P("dom", None),
        P("dom", None),
        P("dom", None, None, None),
    )
    return jax.shard_map(
        shards,
        mesh=mesh,
        in_specs=placed,
        out_specs=(P("rep", "dom", None), P("rep", "dom", None), P(), P(), P()),
        check_vma=False,
    )
```

```python
import functools
import math

import jax
import jax.numpy as jnp
from jax import lax
from jax.experimental import pallas as pl
from jax.experimental.pallas import tpu as pltpu
from jax.sharding import PartitionSpec as P

F32 = jnp.float32
BF16 = jnp.bfloat16
BLK = 128
VM = pl.BlockSpec(memory_space=pltpu.VMEM)
SM = pl.BlockSpec(memory_space=pltpu.SMEM)
LIMIT = pltpu.CompilerParams(vmem_limit_bytes=56 * 1024 * 1024)


def dot(a, b):
    return jnp.dot(a, b, preferred_element_type=F32)


def dot_t0(a, b):
    return lax.dot_general(a, b, (((0,), (0,)), ((), ())), preferred_element_type=F32)


def dot_t1(a, b):
    return lax.dot_general(a, b, (((1,), (1,)), ((), ())), preferred_element_type=F32)


def pair(k):
    return slice(k * 128, (k + 1) * 128)


def window2(k):
    return slice(k * 128, (k + 2) * 128)


def block_map(weight_ref, index, out_ref):
    c = weight_ref.shape[1]
    w = weight_ref[index]
    out_ref[...] = jnp.zeros(out_ref.shape, BF16)
    out_ref[0:c, 0:c] = w
    out_ref[c : 2 * c, c : 2 * c] = w


def band_blocks(dilation):
    if dilation == 1:
        return ((0, 1, 0), (0, 2, 1), (1, 2, 0), (1, 3, 1))
    return ((0, 0, 0), (0, 1, 1), (1, 2, 0), (1, 3, 1))


def band_map(conv_ref, dilation, out_ref):
    c = conv_ref.shape[1]
    out_ref[...] = jnp.zeros(out_ref.shape, BF16)
    for tap, i, o in band_blocks(dilation):
        w = conv_ref[tap]
        rows = slice(i * c, (i + 1) * c)
        out_ref[rows, o * c : (o + 1) * c] = w[:, :c]
        out_ref[rows, (o + 2) * c : (o + 3) * c] = w[:, c:]


def band_grad(total, dilation, out_ref):
    c = out_ref.shape[1]
    for tap in range(2):
        for half in range(2):
            acc = None
            for t, i, o in band_blocks(dilation):
                if t != tap:
                    continue
                col = (o + 2 * half) * c
                part = total[i * c : (i + 1) * c, col : col + c]
                acc = part if acc is None else acc + part
            out_ref[tap, :, half * c : (half + 1) * c] = acc


def activations(pre):
    filt = jnp.tanh(pre[:, :128])
    gates = 0.5 * jnp.tanh(0.5 * pre[:, 128:]) + 0.5
    return filt, gates


def earlier(ref, k):
    if k == 0:
        x = ref[:, 0:128]
        return jnp.concatenate([jnp.zeros_like(x), x], axis=1)
    return ref[:, window2(k - 1)]


def build_tiles(cols_ref, vals_ref, acc_ref, dense_ref):
    rtiles, slots = vals_ref.shape[0], vals_ref.shape[1]
    ctiles = dense_ref.shape[1] // BLK
    for r in range(rtiles):
        acc_ref[...] = jnp.zeros(acc_ref.shape, F32)
        for j in range(slots):
            c = cols_ref[r, j]
            acc_ref[c] = acc_ref[c] + vals_ref[r, j].astype(F32)
        for c in range(ctiles):
            dense_ref[r * BLK : (r + 1) * BLK, c * BLK : (c + 1) * BLK] = acc_ref[c].astype(BF16)


def build_picks(send_ref, counts_ref, picks_ref):
    parts = send_ref.shape[0]
    nodes = picks_ref.shape[0]
    lane = lax.broadcasted_iota(jnp.int32, (1, BLK), 1)
    rows = lax.broadcasted_iota(jnp.int32, (nodes, BLK), 0)
    for q in range(parts):
        wanted = jnp.where(lane < counts_ref[0, q], send_ref[q : q + 1, :], -1)
        hit = rows == wanted
        picks_ref[:, q * BLK : (q + 1) * BLK] = jnp.where(hit, 1.0, 0.0).astype(BF16)


def prepare_body(cot_ref, mix_ref, send_ref, counts_ref, cols_ref, vals_ref,
                 dense_ref, picks_ref, cot_out, base_ref, pieces_ref,
                 acc_ref, map_ref, g_ref):
    nodes = cot_ref.shape[1]
    parts = send_ref.shape[0]
    c = mix_ref.shape[1]
    build_tiles(cols_ref, vals_ref, acc_ref, dense_ref)
    build_picks(send_ref, counts_ref, picks_ref)
    wide = cot_ref[...].astype(F32).T
    wide = jnp.concatenate([jnp.zeros((nodes, c), F32), wide], axis=1).astype(BF16)
    cot_out[...] = wide
    pairs = cot_out.shape[1] // 128
    block_map(mix_ref, 2, map_ref)
    m = map_ref[...]
    for k in range(pairs):
        g_ref[:, pair(k)] = dot_t1(cot_out[:, pair(k)], m).astype(BF16)
    block_map(mix_ref, 1, map_ref)
    m = map_ref[...]
    g = g_ref[...]
    pack_rows(g, dense_ref, nodes, parts, pieces_ref)
    base_ref[...] = dot_t0(dense_ref[:, :nodes], g)
    for k in range(pairs):
        base_ref[:, pair(k)] += dot_t1(cot_out[:, pair(k)], m)


def pack_rows(values, table_ref, start, parts, out_ref):
    flipped = values.astype(F32).T.astype(BF16)
    for q in range(parts):
        table = table_ref[:, start + q * BLK : start + (q + 1) * BLK]
        out_ref[q] = dot(flipped, table).astype(BF16)


def from_blocks(total, table_ref, start, parts, arrived_ref):
    for q in range(parts):
        table = table_ref[:, start + q * BLK : start + (q + 1) * BLK]
        total = total + dot_t1(table, arrived_ref[q])
    return total


def forward_part(x_ref, conv1_ref, conv2_ref, first_ref, hidden_ref, band_ref):
    pairs = x_ref.shape[1] // 128
    band_map(conv1_ref, 1, band_ref)
    b = band_ref[...]
    for k in range(pairs):
        filt, gates = activations(dot(earlier(x_ref, k), b))
        first_ref[:, pair(k)] = (filt * gates).astype(BF16)
    band_map(conv2_ref, 2, band_ref)
    b = band_ref[...]
    for k in range(1, pairs):
        filt, gates = activations(dot(earlier(first_ref, k), b))
        hidden_ref[:, pair(k - 1)] = (filt * gates).astype(BF16)


def gate_grad(pre, up):
    filt, gates = activations(pre)
    d_filt = up * gates * (1.0 - filt * filt)
    d_gate = up * filt * gates * (1.0 - gates)
    return jnp.concatenate([d_filt, d_gate], axis=1).astype(BF16)


def backward_part(x_ref, first_ref, cot_ref, conv1_ref, conv2_ref, grad_ref, g1_ref, g2_ref,
                  band_ref, up_ref, mid_ref):
    pairs = x_ref.shape[1] // 128
    band_map(conv2_ref, 2, band_ref)
    b = band_ref[...]
    total = None
    carry = None
    for k in range(1, pairs):
        both = earlier(first_ref, k)
        d = gate_grad(dot(both, b), up_ref[:, pair(k - 1)])
        part = dot_t0(both, d)
        total = part if total is None else total + part
        back = dot_t1(d, b)
        low = back[:, :128] if carry is None else carry + back[:, :128]
        mid_ref[:, pair(k - 1)] = low.astype(BF16)
        carry = back[:, 128:]
    mid_ref[:, pair(pairs - 1)] = carry.astype(BF16)
    band_grad(total, 2, g2_ref)
    band_map(conv1_ref, 1, band_ref)
    b = band_ref[...]
    total = None
    carry = None
    for k in range(pairs):
        both = earlier(x_ref, k)
        d = gate_grad(dot(both, b), mid_ref[:, pair(k)].astype(F32))
        part = dot_t0(both, d)
        total = part if total is None else total + part
        back = dot_t1(d, b)
        if k > 0:
            low = carry + back[:, :128]
            if k > 1:
                low = low + cot_ref[:, pair(k - 2)].astype(F32)
            grad_ref[:, pair(k - 1)] = low.astype(BF16)
        carry = back[:, 128:]
    last = carry + cot_ref[:, pair(pairs - 2)].astype(F32)
    grad_ref[:, pair(pairs - 1)] = last.astype(BF16)
    band_grad(total, 1, g1_ref)


def mix_grad(term_ref, cot_ref, c):
    acc = None
    for k in range(cot_ref.shape[1] // 128):
        part = dot_t0(term_ref[:, pair(k)], cot_ref[:, pair(k)])
        acc = part if acc is None else acc + part
    return acc[:c, :c] + acc[c:, c:]


def early_part(hidden_ref, hop_ref, x_ref, cot_ref, mix_ref, gm_ref, map0, map1, wide_ref):
    c = mix_ref.shape[1]
    block_map(mix_ref, 0, map0)
    block_map(mix_ref, 1, map1)
    for k in range(cot_ref.shape[1] // 128):
        acc = x_ref[:, pair(k + 1)].astype(F32)
        acc = acc + dot(hidden_ref[:, pair(k)], map0[...])
        wide_ref[:, pair(k)] = acc + dot(hop_ref[:, pair(k)], map1[...])
    gm_ref[0] = mix_grad(hidden_ref, cot_ref, c)
    gm_ref[1] = mix_grad(hop_ref, cot_ref, c)


def main_body(parts, reps, scale,
              x_ref, cot_ref, conv1_ref, conv2_ref, mix_ref, dense_ref, picks_ref, base_ref,
              pieces_ref,
              out_ref, grad_ref, sum_ref,
              first_ref, hidden_ref, hop_ref, second_ref, up_ref, mid_ref, band_ref,
              map0, map1, map2, g1_ref, g2_ref, gm_ref,
              wide_ref, send1, send2, send3, recv0, recv1, recv2, recv3,
              pack_ref, got_ref, part_ref, reps_ref, sums_ref,
              ssem, rsem, asem, arsem, bsem, brsem):
    me = lax.axis_index("dom")
    mine = lax.axis_index("rep")
    nodes = x_ref.shape[0]
    c = mix_ref.shape[1]
    pairs = cot_ref.shape[1] // 128
    feats = cot_ref.shape[1]

    barrier = pltpu.get_barrier_semaphore()
    for o in range(1, parts):
        pl.semaphore_signal(barrier, inc=1, device_id={"dom": lax.rem(me + o, parts)},
                            device_id_type=pl.DeviceIdType.MESH)
    for o in range(1, reps):
        pl.semaphore_signal(barrier, inc=1, device_id={"rep": lax.rem(mine + o, reps)},
                            device_id_type=pl.DeviceIdType.MESH)
    pl.semaphore_wait(barrier, parts - 1 + reps - 1)

    def copies(level, src, dst):
        made = []
        for o in sorted(range(1, parts), key=lambda o: abs(2 * o - parts)):
            peer = lax.rem(me + o, parts)
            made.append(pltpu.make_async_remote_copy(
                src_ref=src.at[peer, pl.ds(c, feats - c)],
                dst_ref=dst.at[me, pl.ds(c, feats - c)],
                send_sem=ssem.at[level, o],
                recv_sem=rsem.at[level, o],
                device_id={"dom": peer},
                device_id_type=pl.DeviceIdType.MESH,
            ))
        for m in made:
            m.start()
        return made

    def arrive(made):
        for m in made:
            m.wait_recv()

    round0 = copies(0, pieces_ref, recv0)
    for buf in (recv0, recv1, recv2, recv3):
        buf[:, 0:c, :] = jnp.zeros((parts, c, BLK), BF16)
        buf[me] = jnp.zeros((feats, BLK), BF16)

    forward_part(x_ref, conv1_ref, conv2_ref, first_ref, hidden_ref, band_ref)
    pack_rows(hidden_ref[...], picks_ref, 0, parts, send1)
    round1 = copies(1, send1, recv1)

    arrive(round0)
    g = from_blocks(base_ref[...], picks_ref, 0, parts, recv0).astype(BF16)
    pack_rows(g, dense_ref, nodes, parts, send2)
    round2 = copies(2, send2, recv2)
    up_ref[...] = dot_t0(dense_ref[:, :nodes], g)
    block_map(mix_ref, 0, map0)
    for k in range(pairs):
        up_ref[:, pair(k)] += dot_t1(cot_ref[:, pair(k)], map0[...])

    own = dot(dense_ref[:, :nodes], hidden_ref[...])
    arrive(round1)
    hop_ref[...] = from_blocks(own, dense_ref, nodes, parts, recv1).astype(BF16)
    pack_rows(hop_ref[...], picks_ref, 0, parts, send3)
    round3 = copies(3, send3, recv3)

    arrive(round2)
    up_ref[...] = from_blocks(up_ref[...], picks_ref, 0, parts, recv2)
    backward_part(x_ref, first_ref, cot_ref, conv1_ref, conv2_ref, grad_ref, g1_ref, g2_ref,
                  band_ref, up_ref, mid_ref)

    early_part(hidden_ref, hop_ref, x_ref, cot_ref, mix_ref, gm_ref, map0, map1, wide_ref)
    block_map(mix_ref, 2, map2)
    own = dot(dense_ref[:, :nodes], hop_ref[...])
    arrive(round3)
    second_ref[...] = from_blocks(own, dense_ref, nodes, parts, recv3).astype(BF16)
    gm_ref[2] = mix_grad(second_ref, cot_ref, c)

    per = pack_ref.shape[1]
    flat = pack_ref
    flat[...] = jnp.zeros(flat.shape, F32)

    def put(first_row, value):
        rows = value.shape[0]
        done = 0
        while done < rows:
            slot, at = divmod(first_row + done, per)
            step = min(per - at, rows - done)
            flat[slot, at : at + step, :] = value[done : done + step]
            done += step

    put(0, g1_ref[0])
    put(c, g1_ref[1])
    put(2 * c, g2_ref[0])
    put(3 * c, g2_ref[1])
    put(4 * c, jnp.concatenate([gm_ref[0], gm_ref[1]], axis=1))
    put(5 * c, jnp.concatenate([gm_ref[2], jnp.zeros((c, c), F32)], axis=1))

    scatter = []
    for o in range(1, parts):
        peer = lax.rem(me + o, parts)
        scatter.append(pltpu.make_async_remote_copy(
            src_ref=pack_ref.at[peer], dst_ref=got_ref.at[me],
            send_sem=asem.at[0, o], recv_sem=arsem.at[0, o],
            device_id={"dom": peer}, device_id_type=pl.DeviceIdType.MESH))
    for m in scatter:
        m.start()
    for k in range(pairs):
        wide_ref[:, pair(k)] += dot(second_ref[:, pair(k)], map2[...])
    out_ref[...] = wide_ref[...].T[c:].astype(BF16)
    got_ref[me] = pack_ref[me]
    arrive(scatter)
    total = got_ref[0]
    for q in range(1, parts):
        total = total + got_ref[q]
    part_ref[...] = total
    around = []
    for o in range(1, reps):
        peer = lax.rem(mine + o, reps)
        around.append(pltpu.make_async_remote_copy(
            src_ref=part_ref, dst_ref=reps_ref.at[mine],
            send_sem=bsem.at[o], recv_sem=brsem.at[o],
            device_id={"rep": peer}, device_id_type=pl.DeviceIdType.MESH))
    for m in around:
        m.start()
    reps_ref[mine] = total
    arrive(around)
    total = reps_ref[0]
    for q in range(1, reps):
        total = total + reps_ref[q]
    for m in around:
        m.wait_send()
    part_ref[...] = total * (1.0 / scale)
    final = []
    for o in range(1, parts):
        peer = lax.rem(me + o, parts)
        final.append(pltpu.make_async_remote_copy(
            src_ref=part_ref, dst_ref=sums_ref.at[me],
            send_sem=asem.at[1, o], recv_sem=arsem.at[1, o],
            device_id={"dom": peer}, device_id_type=pl.DeviceIdType.MESH))
    for m in final:
        m.start()
    sums_ref[me] = part_ref[...]
    arrive(final)

    sum_ref[...] = sums_ref[...]
    for m in round0 + round1 + round2 + round3 + scatter + final:
        m.wait_send()


def shards(inputs, cotangent, conv_one, conv_two, mix_weight, send_rows, counts, tile_cols,
           tile_vals):
    windows, nodes, flat = inputs.shape
    channels = mix_weight.shape[1]
    parts = lax.axis_size("dom")
    reps = lax.axis_size("rep")
    kept = flat // channels - 3
    wide = flat - 2 * channels
    halo = parts * BLK
    blocks = (parts, wide, BLK)
    prepared = [((nodes, nodes + halo), BF16), ((nodes, halo), BF16), ((nodes, wide), BF16),
                ((nodes, wide), F32), (blocks, BF16)]
    dense, picks, cot_wide, base, pieces = pl.pallas_call(
        prepare_body,
        out_shape=[jax.ShapeDtypeStruct(s, d) for s, d in prepared],
        in_specs=[VM, VM, VM, SM, SM, VM],
        out_specs=[VM] * 5,
        scratch_shapes=[pltpu.VMEM((parts + nodes // BLK, BLK, BLK), F32),
                        pltpu.VMEM((128, 128), BF16), pltpu.VMEM((nodes, wide), BF16)],
        compiler_params=LIMIT,
        name="prepare",
    )(cotangent[0].T, mix_weight, send_rows[0], counts, tile_cols, tile_vals)
    scaling = math.sqrt(float(windows * reps * nodes * parts * kept))
    unit = 8 * parts
    per = -(-6 * channels // unit) * unit // parts
    results = [((kept * channels, nodes), BF16), ((nodes, flat), BF16), ((parts, per, BLK), F32)]
    scratch = [((nodes, flat), BF16), ((nodes, wide), BF16), ((nodes, wide), BF16),
               ((nodes, wide), BF16), ((nodes, wide), F32), ((nodes, flat), BF16),
               ((256, 256), BF16), ((128, 128), BF16), ((128, 128), BF16), ((128, 128), BF16),
               (conv_one.shape, F32), (conv_two.shape, F32), (mix_weight.shape, F32)]
    scratch += [((nodes, wide), F32)] + [(blocks, BF16)] * 7
    scratch += [((parts, per, BLK), F32), ((parts, per, BLK), F32), ((per, BLK), F32),
                ((reps, per, BLK), F32), ((parts, per, BLK), F32)]
    dma = pltpu.SemaphoreType.DMA
    output, grad_input, packed = pl.pallas_call(
        functools.partial(main_body, parts, reps, scaling),
        out_shape=[jax.ShapeDtypeStruct(s, d) for s, d in results],
        in_specs=[VM] * 9,
        out_specs=[VM] * 3,
        scratch_shapes=[pltpu.VMEM(s, d) for s, d in scratch]
        + [dma((4, parts)), dma((4, parts)), dma((2, parts)), dma((2, parts)), dma((reps,)),
           dma((reps,))],
        compiler_params=pltpu.CompilerParams(
            vmem_limit_bytes=60 * 1024 * 1024, collective_id=0, has_side_effects=True),
        name="layer",
    )(inputs[0], cot_wide, conv_one, conv_two, mix_weight, dense, picks, base, pieces)
    c = channels
    rows = packed.reshape(parts * per, BLK)
    gm = jnp.stack([rows[4 * c : 5 * c, :c], rows[4 * c : 5 * c, c:], rows[5 * c : 6 * c, :c]])
    return (
        output.T[None],
        grad_input[None],
        rows[: 2 * c].reshape(conv_one.shape),
        rows[2 * c : 4 * c].reshape(conv_two.shape),
        gm,
    )


def solution(mesh):
    placed = (
        P("rep", "dom", None),
        P("rep", "dom", None),
        P(),
        P(),
        P(),
        P("dom", None, None),
        P("dom", None),
        P("dom", None),
        P("dom", None, None, None),
    )
    return jax.shard_map(
        shards,
        mesh=mesh,
        in_specs=placed,
        out_specs=(P("rep", "dom", None), P("rep", "dom", None), P(), P(), P()),
        check_vma=False,
    )
```
